32 devices in a mesh: dp: 2 (over y), pipe: 4 (over x, core), seq: 4 (over z).
Axes of the slice: x: 2, y: 2, z: 4, core: 2. Of those that a mesh axis runs over, the one named last changes fastest.
Arguments:
- query_states: bfloat16 [8, 512, 8192], P(('dp', 'pipe'), 'seq'), parts along dimension 0, may hold values from -15 to 15
- projected_keys: bfloat16 [8, 512, 1024], P(('dp', 'pipe'), 'seq'), parts along dimension 0, may hold values from -8 to 8
- projected_values: bfloat16 [8, 512, 1024], P(('dp', 'pipe'), 'seq'), parts along dimension 0, may hold values from -6 to 6
- positions: int32 [8, 512], P(('dp', 'pipe'), 'seq'), parts along dimension 0, may hold values from 0 to 1023, as said below
- segments: int32 [8, 512], P(('dp', 'pipe'), 'seq'), parts along dimension 0, may hold values from 0 to 3, as said below
Outputs:
- handed: bfloat16 [8, 512, 8192], P(('dp', 'pipe'), 'seq'), parts along dimension 0
The draws below stay inside these ranges and needn't reach their ends.
There are 2 independent parts, one for each index of `dp`. The reference program is written for one: setup_inputs(seed, part) draws one part's arguments, and reference() takes and returns one part's arrays. A program takes and returns all parts, laid end to end along the dimension named above; each array names one. Nothing has to cross between parts.
Inputs may be any that keep to these rules, and one draw needn't show every extreme that they name: `segments`: within each micro-batch ids never fall along the sequence, start at 0, every id occurs, and every document holds 4 or more tokens. `positions`: within a document a position is one more than the previous token's; the first document of each micro-batch starts at 0, and the last token of each micro-batch has position 1023.
All inputs are finite; a program needn't handle non-finite values.
Results may differ from the reference program's by a relative error of at most 0.0014.
The reference program's roundings to bfloat16 on the way count: a program that leaves them out, or rounds other values in their place, can miss the bound.
Values may be sent and summed in bfloat16 or wider, within the bound.
No kernel may reach another device: no remote copies, remote signals or barrier semaphores. Data moves between devices by JAX's collectives and lax.ppermute only.
A program may use at most 64 MiB of HBM per device.

```python
import math
import jax
import jax.numpy as jnp
from jax import lax

QUERY_HEADS = 64
KEY_VALUE_HEADS = 8
HEAD_SIZE = 128
DOCS = 4
SECTION_TOKENS = 512
RELAY_SECTIONS = 4


def doc_layout(key):
    section_keys = jax.random.split(jax.random.fold_in(key, 11), RELAY_SECTIONS)

    def one_section(section_key):
        perm_key, offset_key = jax.random.split(section_key)
        shuffled = jax.random.permutation(perm_key, SECTION_TOKENS // 4 - 1)
        doc_starts = ((shuffled[:DOCS - 1] + 1) * 4).astype(jnp.int32)
        row_index = jnp.arange(SECTION_TOKENS, dtype=jnp.int32)
        opening = jnp.any(row_index[:, None] == doc_starts[None, :], axis=1)
        segment_ids = jnp.cumsum(opening.astype(jnp.int32)).astype(jnp.int32)
        begins = lax.cummax(jnp.where(opening, row_index, 0), axis=0)
        last_begin = jnp.max(doc_starts).astype(jnp.int32)
        doc_shifts = jax.random.randint(offset_key, (DOCS,), 0, SECTION_TOKENS, dtype=jnp.int32).at[0].set(0)
        doc_shifts = doc_shifts.at[DOCS - 1].set(SECTION_TOKENS + last_begin)
        owner_table = segment_ids[:, None] == jnp.arange(DOCS, dtype=jnp.int32)[None, :]
        doc_offset = jnp.sum(jnp.where(owner_table, doc_shifts[None, :], 0), axis=1)
        spike_rows = jnp.concatenate([jnp.array([2], jnp.int32), doc_starts + 2])
        return (segment_ids, (row_index - begins + doc_offset).astype(jnp.int32), spike_rows)
    return jax.vmap(one_section)(section_keys)


def spike_info(spike_rows, row_lag):
    strength_table = jnp.array([0.5, 1.0, 1.875, 1.875], jnp.float32)[jnp.arange(DOCS) % 4]
    sign_table = jnp.array([1.0, 1.0, 1.0, -1.0], jnp.float32)[jnp.arange(DOCS) % 4]
    row_index = jnp.arange(SECTION_TOKENS, dtype=jnp.int32)
    matches = row_index[None, :, None] == (spike_rows - row_lag)[:, None, :]
    signed = strength_table * sign_table
    strength = jnp.sum(jnp.where(matches, signed[None, None, :], 0.0), axis=-1)
    return (strength, jnp.any(matches, axis=-1))


def spike_dimensions():
    half_dim = HEAD_SIZE // 2
    quarter = max(1, half_dim // 4)
    dim_index = jnp.arange(HEAD_SIZE, dtype=jnp.int32)
    return dim_index % half_dim >= half_dim - quarter


def draw_segments(key, part):
    segment_ids, positions, spike_rows = doc_layout(key)
    return segment_ids


def draw_positions(key, part):
    segment_ids, positions, spike_rows = doc_layout(key)
    return positions


def draw_query_states(key, part):
    segment_ids, positions, spike_rows = doc_layout(key)
    array_shape = (RELAY_SECTIONS, SECTION_TOKENS, QUERY_HEADS * HEAD_SIZE)
    base = jnp.clip(jax.random.normal(jax.random.fold_in(key, 21), array_shape, jnp.float32), -4.0, 4.0)
    strength, hit = spike_info(spike_rows, 0)
    dimension_mask = jnp.tile(spike_dimensions(), QUERY_HEADS)
    spiked = jnp.where(dimension_mask[None, None, :], 8.0 * strength[..., None], 0.0)
    return jnp.where(hit[..., None], spiked, base).astype(jnp.bfloat16)


def draw_projected_keys(key, part):
    segment_ids, positions, spike_rows = doc_layout(key)
    array_shape = (RELAY_SECTIONS, SECTION_TOKENS, KEY_VALUE_HEADS * HEAD_SIZE)
    base = jnp.clip(jax.random.normal(jax.random.fold_in(key, 31), array_shape, jnp.float32), -4.0, 4.0)
    dim_count = 2 * max(1, HEAD_SIZE // 2 // 4)
    attn_gain = 0.1 * math.log(4.0) + 1.0
    unit_score = attn_gain * attn_gain * 64.0 * dim_count / math.sqrt(HEAD_SIZE)
    strength, hit = spike_info(spike_rows, 0)
    strength_prev, hit_prev = spike_info(spike_rows, 1)
    sign_now = jnp.sign(strength)
    sign_prev = jnp.sign(strength_prev)
    size_prev = jnp.maximum(jnp.abs(strength_prev), 0.5)
    near_value = 8.0 * sign_prev * (1.0 - 2.0 / (unit_score * size_prev))
    dimension_mask = jnp.tile(spike_dimensions(), KEY_VALUE_HEADS)[None, None, :]
    result = jnp.where(hit[..., None] & dimension_mask, 8.0 * sign_now[..., None], base)
    result = jnp.where(hit_prev[..., None] & dimension_mask, near_value[..., None], result)
    return result.astype(jnp.bfloat16)


def steps_of(rng, shape, shards, least, largest):
    loudness = 1.0
    for dim, blocks in shards:
        steps = jax.random.uniform(jax.random.fold_in(jax.random.fold_in(rng, 6), dim), (blocks,), jnp.float32, least / len(shards), largest / len(shards))
        loudness = loudness * jnp.repeat(jnp.exp(steps), shape[dim] // blocks).reshape((-1,) + (1,) * (len(shape) - 1 - dim))
    return loudness


def gaussian(key, dims, deviation, limit, cuts=(), held_as=jnp.bfloat16):
    gain = steps_of(key, dims, cuts, -0.22, 0.18) if cuts else 1.0
    drawn = jax.random.normal(key, dims, jnp.float32) * deviation * gain
    return jnp.minimum(jnp.maximum(drawn, -limit), limit).astype(held_as)


def setup_inputs(seed: int = 0, part: int = 0) -> dict:
    splits = jax.random.split(jax.random.key(seed), 6)
    part_keys = jax.random.split(jax.random.fold_in(splits[5], part), 6)
    query_states = draw_query_states(jax.random.fold_in(jax.random.fold_in(splits[5], part), 71), part)
    projected_keys = draw_projected_keys(jax.random.fold_in(jax.random.fold_in(splits[5], part), 71), part)
    projected_values = gaussian(part_keys[2], (RELAY_SECTIONS, SECTION_TOKENS, KEY_VALUE_HEADS * HEAD_SIZE), 1.0, 6.0, ((0, 4), (1, 4)))
    positions = draw_positions(jax.random.fold_in(jax.random.fold_in(splits[5], part), 71), part)
    segments = draw_segments(jax.random.fold_in(jax.random.fold_in(splits[5], part), 71), part)
    return dict(query_states=query_states, projected_keys=projected_keys, projected_values=projected_values, positions=positions, segments=segments)


rope_theta = 1000000.0
yarn_factor = 4.0
trained_length = 32768.0
fast_beta = 32.0
slow_beta = 1.0
masked_score = -1e+30

def yarn_tables(positions, head_dim):
    half_dim = head_dim // 2
    pair_index = jnp.arange(half_dim, dtype=jnp.float32)
    base_freq = 1.0 / rope_theta ** (2.0 * pair_index / head_dim)
    lower = math.floor(head_dim * math.log(trained_length / (fast_beta * 2.0 * math.pi)) / (2.0 * math.log(rope_theta)))
    upper = math.ceil(head_dim * math.log(trained_length / (slow_beta * 2.0 * math.pi)) / (2.0 * math.log(rope_theta)))
    lower = max(lower, 0)
    upper = min(upper, head_dim - 1)
    upper = max(upper, lower + 1)
    ramp_value = jnp.clip((pair_index - lower) / (upper - lower), 0.0, 1.0)
    keep_share = 1.0 - ramp_value
    inv_freq = base_freq / yarn_factor * (1.0 - keep_share) + base_freq * keep_share
    attn_gain = 0.1 * math.log(yarn_factor) + 1.0
    angles = positions.astype(jnp.float32)[..., None] * inv_freq
    return (jnp.cos(angles) * attn_gain, jnp.sin(angles) * attn_gain)

def apply_rotation(states, cosine_table, sine_table):
    half_dim = states.shape[-1] // 2
    first_half = states[..., :half_dim]
    second_half = states[..., half_dim:]
    return jnp.concatenate([first_half * cosine_table - second_half * sine_table, second_half * cosine_table + first_half * sine_table], axis=-1)

def attend_section(rotated_queries, rotated_keys, value_head_rows, segment_ids):
    sequence_total = rotated_queries.shape[0]
    group_size = QUERY_HEADS // KEY_VALUE_HEADS
    block = min(512, sequence_total)
    grouped_queries = rotated_queries.reshape(sequence_total, KEY_VALUE_HEADS, group_size, HEAD_SIZE)
    key_wide = rotated_keys.astype(jnp.float32)
    value_wide = value_head_rows.astype(jnp.float32)
    key_ids = jnp.arange(sequence_total, dtype=jnp.int32)

    def one_block(first_row):
        query_block = lax.dynamic_slice_in_dim(grouped_queries, first_row, block, 0).astype(jnp.float32)
        scores = jnp.einsum('qkgd,nkd->kgqn', query_block, key_wide) / math.sqrt(HEAD_SIZE)
        query_ids = first_row + jnp.arange(block, dtype=jnp.int32)
        query_segs = lax.dynamic_slice_in_dim(segment_ids, first_row, block, 0)
        visible = (key_ids[None, :] <= query_ids[:, None]) & (segment_ids[None, :] == query_segs[:, None])
        scores = jnp.where(visible[None, None], scores, masked_score)
        row_best = lax.optimization_barrier(jnp.max(scores, axis=-1, keepdims=True))
        weights = jnp.where(visible[None, None], jnp.exp(scores - row_best), 0.0)
        totals = lax.optimization_barrier(jnp.sum(weights, axis=-1))
        rounded = weights.astype(jnp.bfloat16).astype(jnp.float32)
        summed = jnp.einsum('kgqn,nkd->qkgd', rounded, value_wide)
        result = summed / jnp.transpose(totals, (2, 0, 1))[..., None]
        return result.reshape(block, QUERY_HEADS * HEAD_SIZE).astype(jnp.bfloat16)
    starts = jnp.arange(sequence_total // block, dtype=jnp.int32) * block
    blocks_out = lax.map(one_block, starts)
    return blocks_out.reshape(sequence_total, QUERY_HEADS * HEAD_SIZE)

def reference(query_states, projected_keys, projected_values, positions, segments):
    cosine_table, sine_table = yarn_tables(positions, HEAD_SIZE)
    cosine_table = cosine_table[:, :, None, :]
    sine_table = sine_table[:, :, None, :]
    rotated_queries = apply_rotation(query_states.astype(jnp.float32).reshape(RELAY_SECTIONS, SECTION_TOKENS, QUERY_HEADS, HEAD_SIZE), cosine_table, sine_table).astype(jnp.bfloat16)
    rotated_keys = apply_rotation(projected_keys.astype(jnp.float32).reshape(RELAY_SECTIONS, SECTION_TOKENS, KEY_VALUE_HEADS, HEAD_SIZE), cosine_table, sine_table).astype(jnp.bfloat16)
    value_head_rows = projected_values.reshape(RELAY_SECTIONS, SECTION_TOKENS, KEY_VALUE_HEADS, HEAD_SIZE)
    attended = jnp.stack([attend_section(rotated_queries[section], rotated_keys[section], value_head_rows[section], segments[section]) for section in range(RELAY_SECTIONS)])
    return jnp.roll(attended, 1, axis=0)
```

```python
import functools
import math

import jax
import jax.numpy as jnp
from jax import lax
from jax.experimental import pallas as pl
from jax.experimental.pallas import tpu as pltpu
from jax.sharding import PartitionSpec as P

QUERY_HEADS = 64
KEY_VALUE_HEADS = 8
HEAD_SIZE = 128
GROUP = QUERY_HEADS // KEY_VALUE_HEADS
WIDTH = GROUP * HEAD_SIZE
SEGMENT_ROWS = 16

rope_theta = 1000000.0
yarn_factor = 4.0
trained_length = 32768.0
fast_beta = 32.0
slow_beta = 1.0
masked_score = -1e30


def yarn_tables(positions, head_dim):
    half_dim = head_dim // 2
    pair_index = jnp.arange(half_dim, dtype=jnp.float32)
    base_freq = 1.0 / rope_theta ** (2.0 * pair_index / head_dim)
    lower = math.floor(
        head_dim
        * math.log(trained_length / (fast_beta * 2.0 * math.pi))
        / (2.0 * math.log(rope_theta))
    )
    upper = math.ceil(
        head_dim
        * math.log(trained_length / (slow_beta * 2.0 * math.pi))
        / (2.0 * math.log(rope_theta))
    )
    lower = max(lower, 0)
    upper = min(upper, head_dim - 1)
    upper = max(upper, lower + 1)
    ramp_value = jnp.clip((pair_index - lower) / (upper - lower), 0.0, 1.0)
    keep_share = 1.0 - ramp_value
    inv_freq = base_freq / yarn_factor * (1.0 - keep_share) + base_freq * keep_share
    attn_gain = 0.1 * math.log(yarn_factor) + 1.0
    angles = positions.astype(jnp.float32)[..., None] * inv_freq
    return (jnp.cos(angles) * attn_gain, jnp.sin(angles) * attn_gain)


def rotated(states, cosine, sine):
    wide = states.astype(jnp.float32)
    return (wide * cosine + pltpu.roll(wide, HEAD_SIZE // 2, 1) * sine).astype(jnp.bfloat16)


def wide_tables(cos_ref, sin_ref):
    cosine, sine = cos_ref[...], sin_ref[...]
    return jnp.concatenate([cosine, cosine], axis=1), jnp.concatenate([-sine, sine], axis=1)


def pack_kernel(groups, keys_ref, values_ref, segment_ref, cos_ref, sin_ref, *packed):
    cosine, sine = wide_tables(cos_ref, sin_ref)
    rows = keys_ref.shape[0]
    ids = segment_ref[...].astype(jnp.float32).astype(jnp.bfloat16)
    first = 0
    for count, out_ref in zip(groups, packed):
        for g in range(count):
            columns = slice((first + g) * HEAD_SIZE, (first + g + 1) * HEAD_SIZE)
            out_ref[g * rows : (g + 1) * rows, :] = rotated(keys_ref[:, columns], cosine, sine)
            out_ref[(count + g) * rows : (count + g + 1) * rows, :] = values_ref[:, columns]
        out_ref[2 * count * rows :, :] = jnp.broadcast_to(ids, (SEGMENT_ROWS, rows))
        first += count


def pack(groups, keys, values, segments, cosine, sine):
    rows = keys.shape[0]
    return pl.pallas_call(
        functools.partial(pack_kernel, groups),
        out_shape=[
            jax.ShapeDtypeStruct((2 * g * rows + SEGMENT_ROWS, HEAD_SIZE), jnp.bfloat16)
            for g in groups
        ],
        name="pack",
        cost_estimate=pl.CostEstimate(
            flops=8 * keys.size, bytes_accessed=8 * keys.size, transcendentals=0
        ),
    )(keys, values, segments, cosine, sine)


def rotate_kernel(queries_ref, cos_ref, sin_ref, out_ref):
    cosine, sine = wide_tables(cos_ref, sin_ref)
    for h in range(GROUP):
        columns = slice(h * HEAD_SIZE, (h + 1) * HEAD_SIZE)
        out_ref[:, columns] = rotated(queries_ref[:, columns], cosine, sine)


def rotate(queries, first, count, cosine, sine):
    rows = queries.shape[0]
    return pl.pallas_call(
        rotate_kernel,
        grid=(count,),
        in_specs=[
            pl.BlockSpec((rows, WIDTH), lambda g: (0, first + g)),
            pl.BlockSpec((rows, HEAD_SIZE // 2), lambda g: (0, 0)),
            pl.BlockSpec((rows, HEAD_SIZE // 2), lambda g: (0, 0)),
        ],
        out_specs=pl.BlockSpec((rows, WIDTH), lambda g: (0, g)),
        out_shape=jax.ShapeDtypeStruct((rows, count * WIDTH), jnp.bfloat16),
        name="rotate",
        cost_estimate=pl.CostEstimate(
            flops=4 * rows * count * WIDTH,
            bytes_accessed=4 * rows * count * WIDTH,
            transcendentals=0,
        ),
    )(queries, cosine, sine)


def attend_kernel(
    before, after, count, blocks, here_ref, *refs
):
    ready = refs[: (before > 0) + (after > 0)]
    refs = refs[len(ready) :]
    queries_ref, payloads = refs[0], refs[1 : 1 + blocks]
    out_ref, bias_ref, keys_ref, values_ref, scores_ref = refs[1 + blocks :]
    step = pl.program_id(0)
    rows = queries_ref.shape[0]
    segment_row = 2 * count * rows

    @pl.when(step == 0)
    def _():
        here = here_ref[0]
        own = payloads[0][segment_row : segment_row + 1, :].astype(jnp.float32)
        query_ids = jnp.broadcast_to(own, (rows, rows)).T
        row = lax.broadcasted_iota(jnp.int32, (rows, rows), 0)
        lane = lax.broadcasted_iota(jnp.int32, (rows, rows), 1)
        for b in range(blocks):
            ids = payloads[b][segment_row : segment_row + 1, :].astype(jnp.float32)
            visible = query_ids == jnp.broadcast_to(ids, (rows, rows))
            ahead = jnp.where(here >= b, -b * rows, (blocks - b) * rows)
            visible = visible & (lane + ahead <= row)
            bias_ref[:, b * rows : (b + 1) * rows] = jnp.where(visible, 0.0, masked_score)

    active = (step >= before) & (step < before + count)

    @pl.when(active)
    def _():
        g = step - before
        for b in range(blocks):
            first = pl.multiple_of(g * rows, rows)
            keys_ref[b * rows : (b + 1) * rows, :] = payloads[b][pl.ds(first, rows), :]
            first = pl.multiple_of((count + g) * rows, rows)
            values_ref[b * rows : (b + 1) * rows, :] = payloads[b][pl.ds(first, rows), :]
        keys = keys_ref[...]
        values = values_ref[...]
        scale = 1.0 / math.sqrt(HEAD_SIZE)
        for h in range(GROUP):
            columns = slice(h * HEAD_SIZE, (h + 1) * HEAD_SIZE)
            scores = lax.dot_general(
                queries_ref[:, columns],
                keys,
                (((1,), (1,)), ((), ())),
                preferred_element_type=jnp.float32,
            )
            scores = scores * scale + bias_ref[...]
            best = jnp.max(scores, axis=1, keepdims=True)
            weights = jnp.exp(scores - best)
            totals = jnp.sum(weights, axis=1, keepdims=True)
            summed = jnp.dot(
                weights.astype(jnp.bfloat16), values, preferred_element_type=jnp.float32
            )
            out_ref[:, columns] = (summed / totals).astype(jnp.bfloat16)

    if before:

        @pl.when(step < before)
        def _():
            out_ref[...] = ready[0][...]

    if after:

        @pl.when(step >= before + count)
        def _():
            out_ref[...] = ready[-1][...]


def attend(queries, payloads, here, ready_before=None, ready_after=None):
    rows = queries.shape[0]
    count = queries.shape[1] // WIDTH
    blocks = len(payloads)
    before = 0 if ready_before is None else ready_before.shape[1] // WIDTH
    after = 0 if ready_after is None else ready_after.shape[1] // WIDTH
    total = before + count + after
    ready, ready_specs = [], []
    if before:
        ready.append(ready_before)
        ready_specs.append(pl.BlockSpec((rows, WIDTH), lambda g, s: (0, jnp.minimum(g, before - 1))))
    if after:
        ready.append(ready_after)
        ready_specs.append(
            pl.BlockSpec((rows, WIDTH), lambda g, s: (0, jnp.maximum(g - before - count, 0)))
        )
    keys = blocks * rows
    return pl.pallas_call(
        functools.partial(attend_kernel, before, after, count, blocks),
        grid_spec=pltpu.PrefetchScalarGridSpec(
            num_scalar_prefetch=1,
            grid=(total,),
            in_specs=[
                *ready_specs,
                pl.BlockSpec((rows, WIDTH), lambda g, s: (0, jnp.clip(g - before, 0, count - 1))),
                *[pl.BlockSpec(p.shape, lambda g, s: (0, 0)) for p in payloads],
            ],
            out_specs=pl.BlockSpec((rows, WIDTH), lambda g, s: (0, g)),
            scratch_shapes=[
                pltpu.VMEM((rows, keys), jnp.float32),
                pltpu.VMEM((keys, HEAD_SIZE), jnp.bfloat16),
                pltpu.VMEM((keys, HEAD_SIZE), jnp.bfloat16),
                pltpu.VMEM((rows, keys), jnp.float32),
            ],
        ),
        out_shape=jax.ShapeDtypeStruct((rows, total * WIDTH), jnp.bfloat16),
        name="attend",
        cost_estimate=pl.CostEstimate(
            flops=4 * rows * keys * count * WIDTH,
            bytes_accessed=4 * rows * count * WIDTH,
            transcendentals=rows * keys * count * GROUP,
        ),
    )(here, *ready, queries, *payloads)


def ring(block, axis):
    size = lax.axis_size(axis)
    return lax.ppermute(block, axis, [(i, (i + 1) % size) for i in range(size)])


CHUNKS = (4, 4)


def on_device(query_states, projected_keys, projected_values, positions, segments):
    cosine, sine = yarn_tables(positions[0], HEAD_SIZE)
    here = lax.axis_index("seq").astype(jnp.int32).reshape(1)
    size = lax.axis_size("seq")
    stay, move = CHUNKS
    pay_stay, pay_move = pack(
        CHUNKS, projected_keys[0], projected_values[0], segments, cosine, sine
    )
    pay_move = ring(pay_move, "pipe")
    stay_blocks, move_blocks = [pay_stay], [pay_move]
    queries_stay = rotate(query_states[0], 0, stay, cosine, sine)
    queries_move = ring(rotate(query_states[0], stay, move, cosine, sine), "pipe")
    for _ in range(size - 1):
        stay_blocks.append(ring(stay_blocks[-1], "seq"))
    for _ in range(size - 1):
        move_blocks.append(ring(move_blocks[-1], "seq"))
    out_stay = ring(attend(queries_stay, stay_blocks, here), "pipe")
    return attend(queries_move, move_blocks, here, ready_before=out_stay)[None]


def solution(mesh):
    placed = (
        P(("dp", "pipe"), "seq", None),
        P(("dp", "pipe"), "seq", None),
        P(("dp", "pipe"), "seq", None),
        P(("dp", "pipe"), "seq"),
        P(("dp", "pipe"), "seq"),
    )
    return jax.shard_map(
        on_device,
        mesh=mesh,
        in_specs=placed,
        out_specs=P(("dp", "pipe"), "seq", None),
        check_vma=False,
    )
```

```python
import functools
import math

import jax
import jax.numpy as jnp
from jax import lax
from jax.experimental import pallas as pl
from jax.experimental.pallas import tpu as pltpu
from jax.sharding import PartitionSpec as P


QUERY_HEADS = 64
KEY_VALUE_HEADS = 8
HEAD_SIZE = 128
GROUP = QUERY_HEADS // KEY_VALUE_HEADS
WIDTH = GROUP * HEAD_SIZE
SEGMENT_ROWS = 16
PAIR = 2

rope_theta = 1000000.0
yarn_factor = 4.0
trained_length = 32768.0
fast_beta = 32.0
slow_beta = 1.0
masked_score = -1e30


def yarn_tables(positions, head_dim):
    half_dim = head_dim // 2
    pair_index = jnp.arange(half_dim, dtype=jnp.float32)
    base_freq = 1.0 / rope_theta ** (2.0 * pair_index / head_dim)
    lower = math.floor(
        head_dim
        * math.log(trained_length / (fast_beta * 2.0 * math.pi))
        / (2.0 * math.log(rope_theta))
    )
    upper = math.ceil(
        head_dim
        * math.log(trained_length / (slow_beta * 2.0 * math.pi))
        / (2.0 * math.log(rope_theta))
    )
    lower = max(lower, 0)
    upper = min(upper, head_dim - 1)
    upper = max(upper, lower + 1)
    ramp_value = jnp.clip((pair_index - lower) / (upper - lower), 0.0, 1.0)
    keep_share = 1.0 - ramp_value
    inv_freq = base_freq / yarn_factor * (1.0 - keep_share) + base_freq * keep_share
    attn_gain = 0.1 * math.log(yarn_factor) + 1.0
    angles = positions.astype(jnp.float32)[..., None] * inv_freq
    return (jnp.cos(angles) * attn_gain, jnp.sin(angles) * attn_gain)


def rotated(states, cosine, sine):
    wide = states.astype(jnp.float32)
    return (wide * cosine + pltpu.roll(wide, HEAD_SIZE // 2, 1) * sine).astype(jnp.bfloat16)


def wide_tables(cos_ref, sin_ref):
    cosine, sine = cos_ref[...], sin_ref[...]
    return jnp.concatenate([cosine, cosine], axis=1), jnp.concatenate([-sine, sine], axis=1)


def pack_kernel(groups, keys_ref, values_ref, segment_ref, cos_ref, sin_ref, *packed):
    cosine, sine = wide_tables(cos_ref, sin_ref)
    rows = keys_ref.shape[0]
    ids = segment_ref[...].astype(jnp.float32).astype(jnp.bfloat16)
    first = 0
    for count, out_ref in zip(groups, packed):
        for g in range(count):
            columns = slice((first + g) * HEAD_SIZE, (first + g + 1) * HEAD_SIZE)
            out_ref[g * rows : (g + 1) * rows, :] = rotated(keys_ref[:, columns], cosine, sine)
            out_ref[(count + g) * rows : (count + g + 1) * rows, :] = values_ref[:, columns]
        out_ref[2 * count * rows :, :] = jnp.broadcast_to(ids, (SEGMENT_ROWS, rows))
        first += count


def pack(groups, keys, values, segments, cosine, sine):
    rows = keys.shape[0]
    return pl.pallas_call(
        functools.partial(pack_kernel, groups),
        out_shape=[
            jax.ShapeDtypeStruct((2 * g * rows + SEGMENT_ROWS, HEAD_SIZE), jnp.bfloat16)
            for g in groups
        ],
        name="pack",
        cost_estimate=pl.CostEstimate(
            flops=8 * keys.size, bytes_accessed=8 * keys.size, transcendentals=0
        ),
    )(keys, values, segments, cosine, sine)


def rotate_kernel(queries_ref, cos_ref, sin_ref, out_ref):
    cosine, sine = wide_tables(cos_ref, sin_ref)
    for h in range(GROUP):
        columns = slice(h * HEAD_SIZE, (h + 1) * HEAD_SIZE)
        out_ref[:, columns] = rotated(queries_ref[:, columns], cosine, sine)


def rotate(queries, first, count, cosine, sine):
    rows = queries.shape[0]
    return pl.pallas_call(
        rotate_kernel,
        grid=(count,),
        in_specs=[
            pl.BlockSpec((rows, WIDTH), lambda g: (0, first + g)),
            pl.BlockSpec((rows, HEAD_SIZE // 2), lambda g: (0, 0)),
            pl.BlockSpec((rows, HEAD_SIZE // 2), lambda g: (0, 0)),
        ],
        out_specs=pl.BlockSpec((rows, WIDTH), lambda g: (0, g)),
        out_shape=jax.ShapeDtypeStruct((rows, count * WIDTH), jnp.bfloat16),
        name="rotate",
        cost_estimate=pl.CostEstimate(
            flops=4 * rows * count * WIDTH,
            bytes_accessed=4 * rows * count * WIDTH,
            transcendentals=0,
        ),
    )(queries, cosine, sine)


def attend_kernel(count, blocks, here_ref, *refs):
    queries_ref, payloads = refs[0], refs[1 : 1 + blocks]
    out_ref, bias_ref, keys_ref, values_ref = refs[-4:]
    step = pl.program_id(0)
    rows = queries_ref.shape[0]
    segment_row = 2 * count * rows

    @pl.when(step == 0)
    def _():
        here = here_ref[0]
        own = payloads[0][segment_row : segment_row + 1, :].astype(jnp.float32)
        query_ids = jnp.broadcast_to(own, (rows, rows)).T
        row = lax.broadcasted_iota(jnp.int32, (rows, rows), 0)
        lane = lax.broadcasted_iota(jnp.int32, (rows, rows), 1)
        for b in range(blocks):
            ids = payloads[b][segment_row : segment_row + 1, :].astype(jnp.float32)
            visible = query_ids == jnp.broadcast_to(ids, (rows, rows))
            ahead = jnp.where(here >= b, -b * rows, (blocks - b) * rows)
            visible = visible & (lane + ahead <= row)
            bias_ref[:, b * rows : (b + 1) * rows] = jnp.where(visible, 0.0, masked_score)

    def attend_group(g):
        for b in range(blocks):
            first = pl.multiple_of(g * rows, rows)
            keys_ref[b * rows : (b + 1) * rows, :] = payloads[b][pl.ds(first, rows), :]
            first = pl.multiple_of((count + g) * rows, rows)
            values_ref[b * rows : (b + 1) * rows, :] = payloads[b][pl.ds(first, rows), :]
        keys = keys_ref[...]
        values = values_ref[...]
        rate = math.log2(math.e) / math.sqrt(HEAD_SIZE)

        def scored(i):
            heads = [
                queries_ref[:, h * HEAD_SIZE : (h + 1) * HEAD_SIZE]
                for h in range(i * PAIR, (i + 1) * PAIR)
            ]
            return lax.dot_general(
                jnp.concatenate(heads, axis=0),
                keys,
                (((1,), (1,)), ((), ())),
                preferred_element_type=jnp.float32,
            )

        def finish(i, rounded, totals):
            summed = jnp.dot(rounded, values, preferred_element_type=jnp.float32)
            result = (summed / totals).astype(jnp.bfloat16)
            for h in range(PAIR):
                columns = slice((i * PAIR + h) * HEAD_SIZE, (i * PAIR + h + 1) * HEAD_SIZE)
                out_ref[:, columns] = result[h * rows : (h + 1) * rows]

        following = scored(0)
        waiting = None
        for i in range(GROUP // PAIR):
            scores = following
            if i + 1 < GROUP // PAIR:
                following = scored(i + 1)
            if waiting is not None:
                finish(*waiting)
            scores = scores.reshape(PAIR, rows, -1) + bias_ref[...][None]
            scores = scores.reshape(PAIR * rows, -1)
            best = jnp.max(scores, axis=1, keepdims=True)
            weights = jnp.exp2((scores - best) * rate)
            totals = jnp.sum(weights, axis=1, keepdims=True)
            waiting = (i, weights.astype(jnp.bfloat16), totals)
        finish(*waiting)

    attend_group(step)


def attend(queries, payloads, here, first, done_before=None):
    rows = queries.shape[0]
    count = queries.shape[1] // WIDTH
    blocks = len(payloads)
    keys = blocks * rows
    so_far = [] if done_before is None else [done_before]
    return pl.pallas_call(
        functools.partial(attend_kernel, count, blocks),
        grid_spec=pltpu.PrefetchScalarGridSpec(
            num_scalar_prefetch=1,
            grid=(count,),
            in_specs=[
                pl.BlockSpec((rows, WIDTH), lambda g, s: (0, g)),
                *[pl.BlockSpec(p.shape, lambda g, s: (0, 0)) for p in payloads],
                *[pl.BlockSpec(memory_space=pl.ANY) for _ in so_far],
            ],
            out_specs=pl.BlockSpec((rows, WIDTH), lambda g, s: (0, first + g)),
            scratch_shapes=[
                pltpu.VMEM((rows, keys), jnp.float32),
                pltpu.VMEM((keys, HEAD_SIZE), jnp.bfloat16),
                pltpu.VMEM((keys, HEAD_SIZE), jnp.bfloat16),
            ],
        ),
        out_shape=jax.ShapeDtypeStruct((rows, KEY_VALUE_HEADS * WIDTH), jnp.bfloat16),
        input_output_aliases={2 + blocks: 0} if so_far else {},
        name="attend",
        cost_estimate=pl.CostEstimate(
            flops=4 * rows * keys * count * WIDTH,
            bytes_accessed=4 * rows * count * WIDTH,
            transcendentals=rows * keys * count * GROUP,
        ),
    )(here, queries, *payloads, *so_far)


def ring(block, axis):
    size = lax.axis_size(axis)
    return lax.ppermute(block, axis, [(i, (i + 1) % size) for i in range(size)])


def ring_both(block):
    sections, size = lax.axis_size("pipe"), lax.axis_size("seq")
    route = [
        (p * size + z, (p + 1) % sections * size + (z + 1) % size)
        for p in range(sections)
        for z in range(size)
    ]
    return lax.ppermute(block, ("pipe", "seq"), route)


CHUNKS = (4, 4)


def on_device(query_states, projected_keys, projected_values, positions, segments):
    cosine, sine = yarn_tables(positions[0], HEAD_SIZE)
    here = lax.axis_index("seq").astype(jnp.int32).reshape(1)
    size = lax.axis_size("seq")
    packed = pack(CHUNKS, projected_keys[0], projected_values[0], segments, cosine, sine)
    held = [[] for _ in CHUNKS]
    for c, payload in enumerate(packed):
        held[c].append(ring(payload, "pipe"))
        held[c].append(ring_both(payload))
        for _ in range(2, size):
            held[c].append(ring(held[c][-1], "seq"))
    result, first = None, 0
    for c, count in enumerate(CHUNKS):
        queries = rotate(query_states[0], first, count, cosine, sine)
        queries = ring(queries, "pipe")
        result = attend(queries, held[c], here, first, result)
        first += count
    return result[None]


def solution(mesh):
    placed = (
        P(("dp", "pipe"), "seq", None),
        P(("dp", "pipe"), "seq", None),
        P(("dp", "pipe"), "seq", None),
        P(("dp", "pipe"), "seq"),
        P(("dp", "pipe"), "seq"),
    )
    return jax.shard_map(
        on_device,
        mesh=mesh,
        in_specs=placed,
        out_specs=P(("dp", "pipe"), "seq", None),
        check_vma=False,
    )
```

```python
import functools
import math

import jax
import jax.numpy as jnp
from jax import lax
from jax.experimental import pallas as pl
from jax.experimental.pallas import tpu as pltpu
from jax.sharding import PartitionSpec as P


QUERY_HEADS = 64
KEY_VALUE_HEADS = 8
HEAD_SIZE = 128
GROUP = QUERY_HEADS // KEY_VALUE_HEADS
WIDTH = GROUP * HEAD_SIZE
SEGMENT_ROWS = 16
PAIR = 2
SMALL_LIMIT = 16 << 20

rope_theta = 1000000.0
yarn_factor = 4.0
trained_length = 32768.0
fast_beta = 32.0
slow_beta = 1.0
masked_score = -1e30


def yarn_frequencies(head_dim):
    half_dim = head_dim // 2
    pair_index = jnp.arange(half_dim, dtype=jnp.float32)
    base_freq = 1.0 / rope_theta ** (2.0 * pair_index / head_dim)
    lower = math.floor(
        head_dim
        * math.log(trained_length / (fast_beta * 2.0 * math.pi))
        / (2.0 * math.log(rope_theta))
    )
    upper = math.ceil(
        head_dim
        * math.log(trained_length / (slow_beta * 2.0 * math.pi))
        / (2.0 * math.log(rope_theta))
    )
    lower = max(lower, 0)
    upper = min(upper, head_dim - 1)
    upper = max(upper, lower + 1)
    ramp_value = jnp.clip((pair_index - lower) / (upper - lower), 0.0, 1.0)
    keep_share = 1.0 - ramp_value
    inv_freq = base_freq / yarn_factor * (1.0 - keep_share) + base_freq * keep_share
    return jnp.concatenate([inv_freq, inv_freq])[None]


def kept_in_hbm(array):
    return pltpu.with_memory_space_constraint(array, pltpu.HBM)


def rotated(states, cosine, sine):
    wide = states.astype(jnp.float32)
    return (wide * cosine + pltpu.roll(wide, HEAD_SIZE // 2, 1) * sine).astype(jnp.bfloat16)


def head_columns(g, width=HEAD_SIZE):
    return slice(g * width, (g + 1) * width)


def pack_kernel(chunks, rates_ref, *refs):
    packed = refs[4 : 4 + len(chunks)]
    cos_ref, sin_ref, positions_ref, segment_ref, keys_ref, values_ref, sems = refs[-7:]
    landed = (positions_ref, segment_ref, keys_ref, values_ref)
    arrivals = [
        pltpu.make_async_copy(source, target, sems.at[i])
        for i, (source, target) in enumerate(zip(refs[:4], landed))
    ]
    for copy in arrivals:
        copy.start()
    rows = keys_ref.shape[0]
    gain = 0.1 * math.log(yarn_factor) + 1.0
    arrivals[0].wait()
    tokens = positions_ref[...].astype(jnp.float32)
    angles = jnp.broadcast_to(tokens, (HEAD_SIZE, rows)).T * rates_ref[...]
    lane = lax.broadcasted_iota(jnp.int32, angles.shape, 1)
    cosine, sine = jnp.cos(angles) * gain, jnp.sin(angles) * gain
    sine = jnp.where(lane < HEAD_SIZE // 2, -sine, sine)
    cos_ref[...], sin_ref[...] = cosine, sine
    for copy in arrivals[1:]:
        copy.wait()
    ids = segment_ref[...].astype(jnp.float32).astype(jnp.bfloat16)
    first = 0
    for count, out_ref in zip(chunks, packed):
        for g in range(count):
            columns = head_columns(first + g)
            out_ref[g * rows : (g + 1) * rows, :] = rotated(keys_ref[:, columns], cosine, sine)
            out_ref[(count + g) * rows : (count + g + 1) * rows, :] = values_ref[:, columns]
        out_ref[2 * count * rows :, :] = jnp.broadcast_to(ids, (SEGMENT_ROWS, rows))
        first += count


def in_vmem(count):
    return [pl.BlockSpec(memory_space=pltpu.VMEM)] * count


def pack(chunks, positions, segments, keys, values):
    rows = keys.shape[0]
    tables = [jax.ShapeDtypeStruct((rows, HEAD_SIZE), jnp.float32)] * 2
    payloads = [
        jax.ShapeDtypeStruct((2 * count * rows + SEGMENT_ROWS, HEAD_SIZE), jnp.bfloat16)
        for count in chunks
    ]
    outs = pl.pallas_call(
        functools.partial(pack_kernel, chunks),
        in_specs=in_vmem(1) + [pl.BlockSpec(memory_space=pl.ANY)] * 4,
        out_specs=in_vmem(len(chunks) + 2),
        out_shape=payloads + tables,
        scratch_shapes=[
            *[pltpu.VMEM(x.shape, x.dtype) for x in (positions, segments, keys, values)],
            pltpu.SemaphoreType.DMA((4,)),
        ],
        compiler_params=pltpu.CompilerParams(vmem_limit_bytes=SMALL_LIMIT),
        name="pack",
        cost_estimate=pl.CostEstimate(
            flops=8 * keys.size, bytes_accessed=8 * keys.size, transcendentals=0
        ),
    )(yarn_frequencies(HEAD_SIZE), *map(kept_in_hbm, (positions, segments, keys, values)))
    return outs[:-2], outs[-2:]


def rotate_kernel(chunks, cos_ref, sin_ref, queries_hbm, *refs):
    outs, (queries_ref, sems) = refs[:-2], refs[-2:]
    cosine, sine = cos_ref[...], sin_ref[...]

    def arrival(g):
        source = queries_hbm.at[:, head_columns(g, WIDTH)]
        return pltpu.make_async_copy(source, queries_ref.at[g], sems.at[g])

    for g in range(sum(chunks)):
        arrival(g).start()
    first = 0
    for count, out_ref in zip(chunks, outs):
        for g in range(count):
            arrival(first + g).wait()
            for h in range(GROUP):
                states = queries_ref[first + g, :, head_columns(h)]
                out_ref[:, head_columns(g * GROUP + h)] = rotated(states, cosine, sine)
        first += count


def rotate(chunks, queries, tables):
    rows = queries.shape[0]
    return pl.pallas_call(
        functools.partial(rotate_kernel, chunks),
        in_specs=in_vmem(2) + [pl.BlockSpec(memory_space=pl.ANY)],
        out_specs=in_vmem(len(chunks)),
        out_shape=[jax.ShapeDtypeStruct((rows, n * WIDTH), jnp.bfloat16) for n in chunks],
        scratch_shapes=[
            pltpu.VMEM((sum(chunks), rows, WIDTH), jnp.bfloat16),
            pltpu.SemaphoreType.DMA((sum(chunks),)),
        ],
        compiler_params=pltpu.CompilerParams(vmem_limit_bytes=SMALL_LIMIT),
        name="rotate",
        cost_estimate=pl.CostEstimate(
            flops=4 * queries.size, bytes_accessed=4 * queries.size, transcendentals=0
        ),
    )(*tables, kept_in_hbm(queries))


def attend_kernel(first, count, size, here_ref, queries_ref, *refs):
    payloads = refs[:size]
    out_hbm, bias_ref, out_ref, sems = refs[-4:]
    rows = queries_ref.shape[0]

    def departure(g):
        start = (first + g) * WIDTH
        start = start if isinstance(g, int) else pl.multiple_of(start, WIDTH)
        target = out_hbm.at[:, pl.ds(start, WIDTH)]
        return pltpu.make_async_copy(out_ref.at[g], target, sems.at[g])

    def ids_of(hop):
        ids = payloads[hop][2 * count * rows : 2 * count * rows + SEGMENT_ROWS, :]
        return jnp.broadcast_to(ids.astype(jnp.float32)[0:1, :], (rows, rows))

    here = here_ref[0]
    query_ids = ids_of(0).T
    row = lax.broadcasted_iota(jnp.int32, (rows, rows), 0)
    lane = lax.broadcasted_iota(jnp.int32, (rows, rows), 1)
    for hop in range(size):
        ahead = jnp.where(here >= hop, -hop * rows, (size - hop) * rows)
        visible = (query_ids == ids_of(hop)) & (lane + ahead <= row)
        bias_ref[:, hop * rows : (hop + 1) * rows] = jnp.where(visible, 0.0, masked_score)

    rate = math.log2(math.e) / math.sqrt(HEAD_SIZE)

    def heads_of(i):
        return range(i * PAIR, (i + 1) * PAIR)

    def attend_group(g, carry):
        def gathered(start):
            start = pl.multiple_of(start * rows, rows)
            return jnp.concatenate([p[pl.ds(start, rows), :] for p in payloads], axis=0)

        keys = gathered(g)
        values = gathered(count + g)

        def scored(i):
            heads = [pl.multiple_of(g * WIDTH + h * HEAD_SIZE, HEAD_SIZE) for h in heads_of(i)]
            return lax.dot_general(
                jnp.concatenate([queries_ref[:, pl.ds(h, HEAD_SIZE)] for h in heads], axis=0),
                keys,
                (((1,), (1,)), ((), ())),
                preferred_element_type=jnp.float32,
            )

        def finish(i, rounded, totals):
            summed = jnp.dot(rounded, values, preferred_element_type=jnp.float32)
            result = (summed / totals).astype(jnp.bfloat16)
            for k, h in enumerate(heads_of(i)):
                out_ref[g, :, head_columns(h)] = result[k * rows : (k + 1) * rows]

        following = scored(0)
        waiting = None
        for i in range(GROUP // PAIR):
            scores = following
            if i + 1 < GROUP // PAIR:
                following = scored(i + 1)
            if waiting is not None:
                finish(*waiting)
            scores = scores.reshape(PAIR, rows, -1) + bias_ref[...][None]
            scores = scores.reshape(PAIR * rows, -1)
            best = jnp.max(scores, axis=1, keepdims=True)
            weights = jnp.exp2((scores - best) * rate)
            totals = jnp.sum(weights, axis=1, keepdims=True)
            waiting = (i, weights.astype(jnp.bfloat16), totals)
        finish(*waiting)
        departure(g).start()
        return carry

    lax.fori_loop(0, count, attend_group, 0)
    for g in range(count):
        departure(g).wait()


def attend(queries, held, here, first=0, onto=None):
    rows = queries.shape[0]
    count = queries.shape[1] // WIDTH
    size = len(held)
    keys = size * rows
    so_far = [] if onto is None else [onto]
    hbm = pl.BlockSpec(memory_space=pl.ANY)
    return pl.pallas_call(
        functools.partial(attend_kernel, first, count, size),
        in_specs=[pl.BlockSpec(memory_space=pltpu.SMEM)] + in_vmem(1 + size) + [hbm] * len(so_far),
        out_specs=hbm,
        out_shape=jax.ShapeDtypeStruct((rows, KEY_VALUE_HEADS * WIDTH), jnp.bfloat16),
        scratch_shapes=[
            pltpu.VMEM((rows, keys), jnp.float32),
            pltpu.VMEM((count, rows, WIDTH), jnp.bfloat16),
            pltpu.SemaphoreType.DMA((count,)),
        ],
        input_output_aliases={2 + size: 0} if so_far else {},
        compiler_params=pltpu.CompilerParams(vmem_limit_bytes=(12 << 20) + 9216 * keys),
        name="attend",
        cost_estimate=pl.CostEstimate(
            flops=4 * rows * keys * count * WIDTH,
            bytes_accessed=4 * rows * count * WIDTH,
            transcendentals=rows * keys * count * GROUP,
        ),
    )(here, queries, *held, *so_far)


def ring(block, axis):
    size = lax.axis_size(axis)
    return lax.ppermute(block, axis, [(i, (i + 1) % size) for i in range(size)])


def ring_both(block):
    sections, size = lax.axis_size("pipe"), lax.axis_size("seq")
    route = [
        (p * size + z, (p + 1) % sections * size + (z + 1) % size)
        for p in range(sections)
        for z in range(size)
    ]
    return lax.ppermute(block, ("pipe", "seq"), route)


CHUNKS = (2, 3, 3)


def on_device(query_states, projected_keys, projected_values, positions, segments):
    here = lax.axis_index("seq").astype(jnp.int32).reshape(1)
    size = lax.axis_size("seq")
    firsts = [sum(CHUNKS[:c]) for c in range(len(CHUNKS))]
    packed, tables = pack(CHUNKS, positions, segments, projected_keys[0], projected_values[0])
    held = []
    for c, payload in enumerate(packed):
        blocks = [ring(payload, "pipe")]
        for hop in range(1, size):
            both = hop == 1 and c in DIAGONAL
            blocks.append(ring_both(payload) if both else ring(blocks[-1], "seq"))
        held.append(blocks)
    turned = rotate(CHUNKS, query_states[0], tables)
    out = None
    for c in range(len(CHUNKS)):
        queries = ring(turned[c], "pipe")
        out = attend(queries, held[c], here, firsts[c], out)
    return out[None]


DIAGONAL = (0, 1, 2)


def solution(mesh):
    placed = (
        P(("dp", "pipe"), "seq", None),
        P(("dp", "pipe"), "seq", None),
        P(("dp", "pipe"), "seq", None),
        P(("dp", "pipe"), "seq"),
        P(("dp", "pipe"), "seq"),
    )
    return jax.shard_map(
        on_device,
        mesh=mesh,
        in_specs=placed,
        out_specs=P(("dp", "pipe"), "seq", None),
        check_vma=False,
    )
```

```python
import functools
import math

import jax
import jax.numpy as jnp
from jax import lax
from jax.experimental import pallas as pl
from jax.experimental.pallas import tpu as pltpu
from jax.sharding import PartitionSpec as P


QUERY_HEADS = 64
KEY_VALUE_HEADS = 8
HEAD_SIZE = 128
GROUP = QUERY_HEADS // KEY_VALUE_HEADS
WIDTH = GROUP * HEAD_SIZE
SEGMENT_ROWS = 16
PAIR = 2
SMALL_LIMIT = 16 << 20

rope_theta = 1000000.0
yarn_factor = 4.0
trained_length = 32768.0
fast_beta = 32.0
slow_beta = 1.0
masked_score = -1e30


def yarn_frequencies(head_dim):
    half_dim = head_dim // 2
    pair_index = jnp.arange(half_dim, dtype=jnp.float32)
    base_freq = 1.0 / rope_theta ** (2.0 * pair_index / head_dim)
    lower = math.floor(
        head_dim
        * math.log(trained_length / (fast_beta * 2.0 * math.pi))
        / (2.0 * math.log(rope_theta))
    )
    upper = math.ceil(
        head_dim
        * math.log(trained_length / (slow_beta * 2.0 * math.pi))
        / (2.0 * math.log(rope_theta))
    )
    lower = max(lower, 0)
    upper = min(upper, head_dim - 1)
    upper = max(upper, lower + 1)
    ramp_value = jnp.clip((pair_index - lower) / (upper - lower), 0.0, 1.0)
    keep_share = 1.0 - ramp_value
    inv_freq = base_freq / yarn_factor * (1.0 - keep_share) + base_freq * keep_share
    return jnp.concatenate([inv_freq, inv_freq])[None]


def kept_in_hbm(array):
    return pltpu.with_memory_space_constraint(array, pltpu.HBM)


def rotated(states, cosine, sine):
    wide = states.astype(jnp.float32)
    return (wide * cosine + pltpu.roll(wide, HEAD_SIZE // 2, 1) * sine).astype(jnp.bfloat16)


def head_columns(g, width=HEAD_SIZE):
    return slice(g * width, (g + 1) * width)


def pack_kernel(chunks, rates_ref, *refs):
    packed = refs[4 : 4 + len(chunks)]
    cos_ref, sin_ref, positions_ref, segment_ref, keys_ref, values_ref, sems = refs[-7:]
    landed = (positions_ref, segment_ref, keys_ref, values_ref)
    arrivals = [
        pltpu.make_async_copy(source, target, sems.at[i])
        for i, (source, target) in enumerate(zip(refs[:4], landed))
    ]
    for copy in arrivals:
        copy.start()
    rows = keys_ref.shape[0]
    gain = 0.1 * math.log(yarn_factor) + 1.0
    arrivals[0].wait()
    tokens = positions_ref[...].astype(jnp.float32)
    angles = jnp.broadcast_to(tokens, (HEAD_SIZE, rows)).T * rates_ref[...]
    lane = lax.broadcasted_iota(jnp.int32, angles.shape, 1)
    cosine, sine = jnp.cos(angles) * gain, jnp.sin(angles) * gain
    sine = jnp.where(lane < HEAD_SIZE // 2, -sine, sine)
    cos_ref[...], sin_ref[...] = cosine, sine
    for copy in arrivals[1:]:
        copy.wait()
    ids = segment_ref[...].astype(jnp.float32).astype(jnp.bfloat16)
    first = 0
    for count, out_ref in zip(chunks, packed):
        for g in range(count):
            columns = head_columns(first + g)
            out_ref[g * rows : (g + 1) * rows, :] = rotated(keys_ref[:, columns], cosine, sine)
            out_ref[(count + g) * rows : (count + g + 1) * rows, :] = values_ref[:, columns]
        out_ref[2 * count * rows :, :] = jnp.broadcast_to(ids, (SEGMENT_ROWS, rows))
        first += count


def in_vmem(count):
    return [pl.BlockSpec(memory_space=pltpu.VMEM)] * count


def pack(chunks, positions, segments, keys, values):
    rows = keys.shape[0]
    tables = [jax.ShapeDtypeStruct((rows, HEAD_SIZE), jnp.float32)] * 2
    payloads = [
        jax.ShapeDtypeStruct((2 * count * rows + SEGMENT_ROWS, HEAD_SIZE), jnp.bfloat16)
        for count in chunks
    ]
    outs = pl.pallas_call(
        functools.partial(pack_kernel, chunks),
        in_specs=in_vmem(1) + [pl.BlockSpec(memory_space=pl.ANY)] * 4,
        out_specs=in_vmem(len(chunks) + 2),
        out_shape=payloads + tables,
        scratch_shapes=[
            *[pltpu.VMEM(x.shape, x.dtype) for x in (positions, segments, keys, values)],
            pltpu.SemaphoreType.DMA((4,)),
        ],
        compiler_params=pltpu.CompilerParams(vmem_limit_bytes=SMALL_LIMIT),
        name="pack",
        cost_estimate=pl.CostEstimate(
            flops=8 * keys.size, bytes_accessed=8 * keys.size, transcendentals=0
        ),
    )(yarn_frequencies(HEAD_SIZE), *map(kept_in_hbm, (positions, segments, keys, values)))
    return outs[:-2], outs[-2:]


def rotate_kernel(chunks, cos_ref, sin_ref, queries_hbm, *refs):
    outs, (queries_ref, sems) = refs[:-2], refs[-2:]
    cosine, sine = cos_ref[...], sin_ref[...]

    def arrival(g):
        source = queries_hbm.at[:, head_columns(g, WIDTH)]
        return pltpu.make_async_copy(source, queries_ref.at[g], sems.at[g])

    for g in range(sum(chunks)):
        arrival(g).start()
    first = 0
    for count, out_ref in zip(chunks, outs):
        for g in range(count):
            arrival(first + g).wait()
            for h in range(GROUP):
                states = queries_ref[first + g, :, head_columns(h)]
                out_ref[:, head_columns(g * GROUP + h)] = rotated(states, cosine, sine)
        first += count


def rotate(chunks, queries, tables):
    rows = queries.shape[0]
    return pl.pallas_call(
        functools.partial(rotate_kernel, chunks),
        in_specs=in_vmem(2) + [pl.BlockSpec(memory_space=pl.ANY)],
        out_specs=in_vmem(len(chunks)),
        out_shape=[jax.ShapeDtypeStruct((rows, n * WIDTH), jnp.bfloat16) for n in chunks],
        scratch_shapes=[
            pltpu.VMEM((sum(chunks), rows, WIDTH), jnp.bfloat16),
            pltpu.SemaphoreType.DMA((sum(chunks),)),
        ],
        compiler_params=pltpu.CompilerParams(vmem_limit_bytes=SMALL_LIMIT),
        name="rotate",
        cost_estimate=pl.CostEstimate(
            flops=4 * queries.size, bytes_accessed=4 * queries.size, transcendentals=0
        ),
    )(*tables, kept_in_hbm(queries))


def attend_kernel(first, count, size, here_ref, queries_ref, *refs):
    payloads = refs[:size]
    if first is None:
        out_ref, bias_ref = refs[-2:]
    else:
        out_hbm, bias_ref, out_ref, sems = refs[-4:]
    rows = queries_ref.shape[0]

    def departure(g):
        start = (first + g) * WIDTH
        start = start if isinstance(g, int) else pl.multiple_of(start, WIDTH)
        target = out_hbm.at[:, pl.ds(start, WIDTH)]
        return pltpu.make_async_copy(out_ref.at[g], target, sems.at[g])

    def ids_of(hop):
        ids = payloads[hop][2 * count * rows : 2 * count * rows + SEGMENT_ROWS, :]
        return jnp.broadcast_to(ids.astype(jnp.float32)[0:1, :], (rows, rows))

    here = here_ref[0]
    query_ids = ids_of(0).T
    row = lax.broadcasted_iota(jnp.int32, (rows, rows), 0)
    lane = lax.broadcasted_iota(jnp.int32, (rows, rows), 1)
    for hop in range(size):
        ahead = jnp.where(here >= hop, -hop * rows, (size - hop) * rows)
        visible = (query_ids == ids_of(hop)) & (lane + ahead <= row)
        bias_ref[:, hop * rows : (hop + 1) * rows] = jnp.where(visible, 0.0, masked_score)

    rate = math.log2(math.e) / math.sqrt(HEAD_SIZE)

    def heads_of(i):
        return range(i * PAIR, (i + 1) * PAIR)

    def attend_group(g, carry):
        def gathered(start):
            start = pl.multiple_of(start * rows, rows)
            return jnp.concatenate([p[pl.ds(start, rows), :] for p in payloads], axis=0)

        keys = gathered(g)
        values = gathered(count + g)

        def scored(i):
            heads = [pl.multiple_of(g * WIDTH + h * HEAD_SIZE, HEAD_SIZE) for h in heads_of(i)]
            return lax.dot_general(
                jnp.concatenate([queries_ref[:, pl.ds(h, HEAD_SIZE)] for h in heads], axis=0),
                keys,
                (((1,), (1,)), ((), ())),
                preferred_element_type=jnp.float32,
            )

        def finish(i, rounded, totals):
            summed = jnp.dot(rounded, values, preferred_element_type=jnp.float32)
            result = (summed / totals).astype(jnp.bfloat16)
            for k, h in enumerate(heads_of(i)):
                out_ref[g, :, head_columns(h)] = result[k * rows : (k + 1) * rows]

        following = scored(0)
        waiting = None
        for i in range(GROUP // PAIR):
            scores = following
            if i + 1 < GROUP // PAIR:
                following = scored(i + 1)
            if waiting is not None:
                finish(*waiting)
            scores = scores.reshape(PAIR, rows, -1) + bias_ref[...][None]
            scores = scores.reshape(PAIR * rows, -1)
            best = jnp.max(scores, axis=1, keepdims=True)
            weights = jnp.exp2((scores - best) * rate)
            totals = jnp.sum(weights, axis=1, keepdims=True)
            waiting = (i, weights.astype(jnp.bfloat16), totals)
        finish(*waiting)
        if first is not None:
            departure(g).start()
        return carry

    lax.fori_loop(0, count, attend_group, 0)
    if first is not None:
        for g in range(count):
            departure(g).wait()


def attend(queries, held, here, first=None, onto=None):
    rows = queries.shape[0]
    count = queries.shape[1] // WIDTH
    size = len(held)
    keys = size * rows
    so_far = [] if onto is None else [onto]
    hbm = pl.BlockSpec(memory_space=pl.ANY)
    if first is None:
        shape, place_spec = (count, rows, WIDTH), in_vmem(1)[0]
        scratch = []
    else:
        shape, place_spec = (rows, KEY_VALUE_HEADS * WIDTH), hbm
        scratch = [
            pltpu.VMEM((count, rows, WIDTH), jnp.bfloat16),
            pltpu.SemaphoreType.DMA((count,)),
        ]
    return pl.pallas_call(
        functools.partial(attend_kernel, first, count, size),
        in_specs=[pl.BlockSpec(memory_space=pltpu.SMEM)] + in_vmem(1 + size) + [hbm] * len(so_far),
        out_specs=place_spec,
        out_shape=jax.ShapeDtypeStruct(shape, jnp.bfloat16),
        scratch_shapes=[pltpu.VMEM((rows, keys), jnp.float32), *scratch],
        input_output_aliases={2 + size: 0} if so_far else {},
        compiler_params=pltpu.CompilerParams(vmem_limit_bytes=(12 << 20) + 9216 * keys),
        name="attend",
        cost_estimate=pl.CostEstimate(
            flops=4 * rows * keys * count * WIDTH,
            bytes_accessed=4 * rows * count * WIDTH,
            transcendentals=rows * keys * count * GROUP,
        ),
    )(here, queries, *(map(kept_in_hbm, held) if first is None else held), *so_far)


def place_kernel(count, block_ref, _, out_hbm, sems):
    copies = [
        pltpu.make_async_copy(
            block_ref.at[g], out_hbm.at[:, head_columns(g, WIDTH)], sems.at[g]
        )
        for g in range(count)
    ]
    for copy in copies:
        copy.start()
    for copy in copies:
        copy.wait()


def place(block, onto):
    count = block.shape[0]
    hbm = pl.BlockSpec(memory_space=pl.ANY)
    return pl.pallas_call(
        functools.partial(place_kernel, count),
        in_specs=in_vmem(1) + [hbm],
        out_specs=hbm,
        out_shape=jax.ShapeDtypeStruct(onto.shape, onto.dtype),
        scratch_shapes=[pltpu.SemaphoreType.DMA((count,))],
        input_output_aliases={1: 0},
        compiler_params=pltpu.CompilerParams(vmem_limit_bytes=SMALL_LIMIT),
        name="place",
        cost_estimate=pl.CostEstimate(
            flops=0, bytes_accessed=4 * block.size, transcendentals=0
        ),
    )(block, onto)


def ring(block, axis):
    size = lax.axis_size(axis)
    return lax.ppermute(block, axis, [(i, (i + 1) % size) for i in range(size)])


def ring_both(block):
    sections, size = lax.axis_size("pipe"), lax.axis_size("seq")
    route = [
        (p * size + z, (p + 1) % sections * size + (z + 1) % size)
        for p in range(sections)
        for z in range(size)
    ]
    return lax.ppermute(block, ("pipe", "seq"), route)


CHUNKS = (2, 3, 3)


def on_device(query_states, projected_keys, projected_values, positions, segments):
    here = lax.axis_index("seq").astype(jnp.int32).reshape(1)
    size = lax.axis_size("seq")
    firsts = [sum(CHUNKS[:c]) for c in range(len(CHUNKS))]
    packed, tables = pack(CHUNKS, positions, segments, projected_keys[0], projected_values[0])
    held = []
    for c, payload in enumerate(packed):
        blocks = [payload]
        for hop in range(1, size):
            both = hop == 1 and c > 0
            blocks.append(ring_both(payload) if both else ring(blocks[-1], "seq"))
        if c > 0:
            blocks[0] = ring(payload, "pipe")
        held.append(blocks)
    turned = rotate(CHUNKS, query_states[0], tables)
    early = attend(turned[0], held[0], here)
    early = ring(early, "pipe")
    out = None
    for c in range(1, len(CHUNKS)):
        queries = ring(turned[c], "pipe")
        out = attend(queries, held[c], here, firsts[c], out)
    out = place(early, out)
    return out[None]


def solution(mesh):
    placed = (
        P(("dp", "pipe"), "seq", None),
        P(("dp", "pipe"), "seq", None),
        P(("dp", "pipe"), "seq", None),
        P(("dp", "pipe"), "seq"),
        P(("dp", "pipe"), "seq"),
    )
    return jax.shard_map(
        on_device,
        mesh=mesh,
        in_specs=placed,
        out_specs=P(("dp", "pipe"), "seq", None),
        check_vma=False,
    )
```
